256 devices in a mesh: embryo: 16 (over z_hi, x), space: 16 (over z_lo, y, core).
Axes of the slice: x: 4, y: 4, z: 8 (z_hi: 4, z_lo: 2; z = z_hi * 2 + z_lo), core: 2. Of those that a mesh axis runs over, the one named last changes fastest.
Arguments:
- density: float32 [16, 256, 256, 128], P('embryo', 'space'), may hold values from 0.1 to 10
- scaling: float32 [16, 256, 256, 128], P('embryo', 'space'), may hold values from 0.5 to 2
- weights: float32 [16], replicated, may hold values from 0.5 to 2
Outputs:
- barycenter: float32 [256, 256, 128], P('space')
- first_scaling: float32 [16, 256, 256, 128], P('embryo', 'space')
- second_scaling: float32 [16, 256, 256, 128], P('embryo', 'space')
The draws below stay inside these ranges and needn't reach their ends.
All inputs are finite; a program needn't handle non-finite values.
Results may differ from the reference program's by a relative error of at most 0.00011.
Values sent between devices are 32-bit elements; how exact they have to be, the bound alone decides.
No kernel may reach another device: no remote copies, remote signals or barrier semaphores. Data moves between devices by JAX's collectives and lax.ppermute only.
A program may use at most 64 MiB of HBM per device.

```python
import math
import jax
import jax.numpy as jnp
from jax import lax

NY = 256
NZ = 128
ITERS = 3
EMBRYOS = 16
NX = 256


def block_levels(rng, dims, pieces, smallest, high):
    def one(dim, shards_of):
        steps = jax.random.uniform(jax.random.fold_in(jax.random.fold_in(rng, 6), dim), (shards_of,), jnp.float32, smallest / len(pieces), high / len(pieces))
        return jnp.repeat(jnp.exp(steps), dims[dim] // shards_of).reshape((-1,) + (1,) * (len(dims) - dim - 1))

    level = one(*pieces[0])
    for cut in pieces[1:]:
        level = level * one(*cut)
    return level


def setup_inputs(seed: int = 0) -> dict:
    streams_of = jax.random.split(jax.random.key(seed), 4)
    density = jnp.clip(jnp.exp(math.log(10.0) - 4.6051702 * jax.random.uniform(streams_of[0], (EMBRYOS, NX, NY, NZ), jnp.float32) ** block_levels(streams_of[0], (EMBRYOS, NX, NY, NZ), ((0, 16), (1, 16)), -0.2, 0.2)), 0.1, 10.0)
    scaling = jnp.clip(jnp.exp(math.log(2.0) - 1.3862944 * jax.random.uniform(streams_of[1], (EMBRYOS, NX, NY, NZ), jnp.float32) ** block_levels(streams_of[1], (EMBRYOS, NX, NY, NZ), ((0, 16), (1, 16)), -0.2, 0.2)), 0.5, 2.0)
    weights = jnp.clip(jnp.exp(jax.random.uniform(streams_of[2], (EMBRYOS,), jnp.float32, math.log(0.5), math.log(2.0))), 0.5, 2.0)
    return {"density": density, "scaling": scaling, "weights": weights}


relax_power = 0.8


def tap_weights():
    offsets = jnp.arange(-6, 7).astype(jnp.float32)
    raw = jnp.exp(-offsets * offsets / 18.0)
    return raw / jnp.sum(raw)


def band_matrix(count):
    row_index = jnp.arange(count)[:, None]
    col_index = jnp.arange(count)[None, :]
    offset = (col_index - row_index).astype(jnp.float32)
    offsets = jnp.arange(-6, 7).astype(jnp.float32)
    total = jnp.sum(jnp.exp(-offsets * offsets / 18.0))
    return jnp.where(jnp.abs(offset) <= 6.0, jnp.exp(-offset * offset / 18.0), 0.0) / total


def kernel_apply(field):
    taps = tap_weights()
    planes = field.shape[0]
    padded = jnp.pad(field, ((6, 6), (0, 0), (0, 0)))
    result = taps[0] * padded[0:planes]
    for shift in range(1, 13):
        result = result + taps[shift] * padded[shift:shift + planes]
    band_y = band_matrix(field.shape[1])
    band_z = band_matrix(field.shape[2])
    result = jnp.einsum('ij,xjz->xiz', band_y, result, precision=lax.Precision.HIGHEST)
    result = jnp.einsum('xyj,kj->xyk', result, band_z, precision=lax.Precision.HIGHEST)
    return result


def one_embryo(pair):
    dens, second = pair
    marginal = kernel_apply(second)
    first = (dens / marginal) ** relax_power
    image = kernel_apply(first)
    return first, image


def reference(density, scaling, weights):
    norm_weights = weights / jnp.sum(weights)
    second = scaling
    for sweep in range(ITERS):
        first, image = lax.map(one_embryo, (density, second))
        logmean = jnp.sum(norm_weights[:, None, None, None] * jnp.log(second * image), axis=0)
        barycenter = jnp.exp(logmean)
        second = (barycenter[None] / image) ** relax_power
    return barycenter, first, second
```

```python
import math

import jax
import jax.numpy as jnp
import numpy as np
from jax import lax
from jax.experimental import pallas as pl
from jax.experimental.pallas import tpu as pltpu
from jax.sharding import PartitionSpec as P

ITERS = 3
RELAX = 0.8
REACH = 6
BF16 = jnp.bfloat16
F32 = jnp.float32


def tap_values():
    raw = np.exp(-np.arange(-REACH, REACH + 1, dtype=np.float64) ** 2 / 18.0)
    return raw / raw.sum()


TAPS = [float(v) for v in tap_values()[REACH:]]


def band(count):
    away = np.abs(np.arange(count)[:, None] - np.arange(count)[None, :])
    full = np.zeros((count, count))
    taps = tap_values()
    for shift in range(REACH + 1):
        full[away == shift] = taps[REACH + shift]
    return full.astype(np.float32)


def two_terms(matrix):
    high = jnp.asarray(matrix).astype(BF16)
    low = (jnp.asarray(matrix) - high.astype(F32)).astype(BF16)
    return high, low


def y_operand(count):
    high, low = two_terms(band(count))
    return jnp.concatenate([high, high, low], axis=1)


def z_operand(count):
    high, low = two_terms(band(count))
    row = jnp.concatenate([high, low], axis=1)
    return jnp.concatenate([row, row], axis=0)


def split(value):
    high = value.astype(BF16)
    return high, (value - high.astype(F32)).astype(BF16)


def x_pass(below, own, above, stacked, planes, rows, lanes):
    def plane(index, at):
        if index < REACH:
            return below[index, at, :]
        if index < REACH + planes:
            return own[index - REACH, at, :]
        return above[index - REACH - planes, at, :]

    def step(tile, carry):
        at = pl.ds(pl.multiple_of(tile * 16, 16), 16)
        at_low = pl.ds(pl.multiple_of(tile * 16 + rows, 16), 16)
        window = [plane(i, at) for i in range(2 * REACH)]
        for p in range(planes):
            window.append(plane(p + 2 * REACH, at))
            total = TAPS[0] * window[REACH]
            for shift in range(1, REACH + 1):
                total = total + TAPS[shift] * (window[REACH - shift] + window[REACH + shift])
            window.pop(0)
            high, low = split(total)
            stacked[at, p * lanes : (p + 1) * lanes] = high
            stacked[at_low, p * lanes : (p + 1) * lanes] = low
        return carry

    lax.fori_loop(0, rows // 16, step, 0)


def yz_pass(stacked, by, bz, planes, rows, lanes, emit):
    def step(pair, carry):
        cols = pl.ds(pl.multiple_of(pair * 2 * lanes, 2 * lanes), 2 * lanes)
        both = stacked[:, cols]
        rhs = jnp.concatenate([both, both[:rows]], axis=0)
        mid = jnp.dot(by[...], rhs, preferred_element_type=F32)
        for half in range(2):
            high, low = split(mid[:, half * lanes : (half + 1) * lanes])
            lhs = jnp.concatenate([high, low], axis=1)
            wide = jnp.dot(lhs, bz[...], preferred_element_type=F32)
            emit(pair * 2 + half, wide[:, :lanes] + wide[:, lanes:])
        return carry

    lax.fori_loop(0, planes // 2, step, 0)


VMEM = pl.BlockSpec(memory_space=pltpu.VMEM)
SMEM = pl.BlockSpec(memory_space=pltpu.SMEM)


def first_kernel(below, own, above, log_density, by, bz, first, stacked):
    planes, rows, lanes = own.shape
    x_pass(below, own, above, stacked, planes, rows, lanes)

    def emit(p, marginal):
        first[p] = jnp.exp(RELAX * (log_density[p] - jnp.log(marginal)))

    yz_pass(stacked, by, bz, planes, rows, lanes, emit)


def image_kernel(places, weight, below, own, above, log_second, by, bz, part, log_image, stacked):
    planes, rows, lanes = own.shape
    half_rows = rows // 2
    x_pass(below, own, above, stacked, planes, rows, lanes)

    def emit(p, image):
        logs = jnp.log(image)
        log_image[p] = logs
        value = weight[0] * (log_second[p] + logs)
        side = p // (planes // 2)
        slot = side * (planes // 2) + ((p % (planes // 2)) ^ places[side])
        for h in range(2):
            start = pl.multiple_of((h ^ places[2 + side]) * half_rows, half_rows)
            part[slot, pl.ds(start, half_rows), :] = value[h * half_rows : (h + 1) * half_rows]

    yz_pass(stacked, by, bz, planes, rows, lanes, emit)


def second_kernel(places, keep_a, more_a, keep_b, more_b, log_image, second, log_second, mean=None):
    quarter, rows, lanes = keep_a.shape
    half_rows = rows // 2
    for side, pieces in enumerate(((keep_a, more_a), (keep_b, more_b))):
        for which, piece in enumerate(pieces):
            for j in range(quarter):
                p = side * 2 * quarter + ((which * quarter + j) ^ places[side])
                for h in range(2):
                    at = pl.ds(pl.multiple_of((h ^ places[2 + side]) * half_rows, half_rows), half_rows)
                    logmean = piece[j, h * half_rows : (h + 1) * half_rows, :]
                    logs = RELAX * (logmean - log_image[p, at, :])
                    second[p, at, :] = jnp.exp(logs)
                    if mean is None:
                        log_second[p, at, :] = logs
                    else:
                        mean[p, at, :] = jnp.exp(logmean)


def last_kernel(places, keep_a, more_a, keep_b, more_b, log_image, second, mean):
    second_kernel(places, keep_a, more_a, keep_b, more_b, log_image, second, None, mean)


def body(density, scaling, weights):
    planes, rows, lanes = density.shape[1:]
    cube = jax.ShapeDtypeStruct((planes, rows, lanes), F32)
    scratch = [pltpu.VMEM((2 * rows, planes * lanes), BF16)]
    by, bz = y_operand(rows), z_operand(lanes)
    count = lax.axis_size("space")
    spot = lax.axis_index("embryo")
    x, z = spot % 4, spot // 4
    mix, top = lambda v: (v & 1) ^ (v >> 1), lambda v: v >> 1
    places = jnp.stack(
        [
            mix(x) * 4 + top(x) * 2 + mix(z),
            top(x) * 4 + mix(x) * 2 + top(z),
            top(z),
            mix(z),
        ]
    ).astype(jnp.int32)
    weight = (weights / jnp.sum(weights))[spot][None]

    cells = planes * rows * lanes
    cost = pl.CostEstimate(flops=cells * 3000, bytes_accessed=cells * 16, transcendentals=cells * 2)

    first_call = pl.pallas_call(
        first_kernel,
        out_shape=cube,
        in_specs=[VMEM] * 6,
        out_specs=VMEM,
        scratch_shapes=scratch,
        cost_estimate=cost,
        name="first",
    )
    image_call = pl.pallas_call(
        image_kernel,
        out_shape=(cube, cube),
        in_specs=[SMEM, SMEM] + [VMEM] * 6,
        out_specs=(VMEM, VMEM),
        scratch_shapes=scratch,
        cost_estimate=cost,
        name="image",
    )
    second_call = pl.pallas_call(
        second_kernel,
        out_shape=(cube, cube),
        in_specs=[SMEM] + [VMEM] * 5,
        out_specs=(VMEM, VMEM),
        name="second",
    )
    last_call = pl.pallas_call(
        last_kernel,
        out_shape=(cube, cube),
        in_specs=[SMEM] + [VMEM] * 5,
        out_specs=(VMEM, VMEM),
        name="last",
    )

    def halo(field):
        up = [(i, i + 1) for i in range(count - 1)]
        down = [(i + 1, i) for i in range(count - 1)]
        below = lax.ppermute(field[planes - REACH :], "space", up)
        above = lax.ppermute(field[:REACH], "space", down)
        return below, above

    def partner_x(mask):
        return [(zz * 4 + i, zz * 4 + (i ^ mask)) for zz in range(4) for i in range(4)]

    def partner_z(mask):
        return [(zz * 4 + i, (zz ^ mask) * 4 + i) for zz in range(4) for i in range(4)]

    def swap(value, perm):
        return lax.ppermute(value, "embryo", perm)

    def all_sum(part):
        half = planes // 2
        sides = []
        plan = (
            (partner_x(1), partner_x(3), partner_z(1), partner_z(3)),
            (partner_x(3), partner_x(1), partner_z(3), partner_z(1)),
        )
        held = [part[:half], part[half:]]
        for stage in range(4):
            sent, kept = [], []
            for value in held:
                if stage < 3:
                    mid = value.shape[0] // 2
                    kept.append(value[:mid])
                    sent.append(value[mid:])
                else:
                    mid = value.shape[1] // 2
                    kept.append(value[:, :mid])
                    sent.append(value[:, mid:])
            sent = lax.optimization_barrier(sent)
            got = lax.optimization_barrier([swap(v, plan[i][stage]) for i, v in enumerate(sent)])
            held = [k + g for k, g in zip(kept, got)]
        for stage in (3, 2, 1, 0):
            held = lax.optimization_barrier(held)
            got = lax.optimization_barrier([swap(v, plan[i][stage]) for i, v in enumerate(held)])
            if stage == 0:
                return held[0], got[0], held[1], got[1]
            axis = 1 if stage == 3 else 0
            held = [jnp.concatenate([k, g], axis=axis) for k, g in zip(held, got)]

    second = scaling[0]
    log_density = jnp.log(density[0])
    log_second = jnp.log(second)
    for sweep in range(ITERS):
        below, above = halo(second)
        first = first_call(below, second, above, log_density, by, bz)
        below, above = halo(first)
        part, log_image = image_call(places, weight, below, first, above, log_second, by, bz)
        pieces = all_sum(part)
        if sweep < ITERS - 1:
            second, log_second = second_call(places, *pieces, log_image)
        else:
            second, mean = last_call(places, *pieces, log_image)
    return mean, first[None], second[None]


def solution(mesh):
    return jax.shard_map(
        body,
        mesh=mesh,
        in_specs=(P("embryo", "space", None, None), P("embryo", "space", None, None), P()),
        out_specs=(
            P("space", None, None),
            P("embryo", "space", None, None),
            P("embryo", "space", None, None),
        ),
        check_vma=False,
    )
```

```python
import math

import jax
import jax.numpy as jnp
import numpy as np
from jax import lax
from jax.experimental import pallas as pl
from jax.experimental.pallas import tpu as pltpu
from jax.sharding import PartitionSpec as P

ITERS = 3
RELAX = 0.8
REACH = 6
BF16 = jnp.bfloat16
F32 = jnp.float32


def tap_values():
    raw = np.exp(-np.arange(-REACH, REACH + 1, dtype=np.float64) ** 2 / 18.0)
    return raw / raw.sum()


TAPS = [float(v) for v in tap_values()[REACH:]]


def band(count):
    away = np.abs(np.arange(count)[:, None] - np.arange(count)[None, :])
    full = np.zeros((count, count))
    taps = tap_values()
    for shift in range(REACH + 1):
        full[away == shift] = taps[REACH + shift]
    return full.astype(np.float32)


def two_terms(matrix):
    high = jnp.asarray(matrix).astype(BF16)
    low = (jnp.asarray(matrix) - high.astype(F32)).astype(BF16)
    return high, low


def y_operand(count):
    high, low = two_terms(band(count))
    return jnp.concatenate([high, high, low], axis=1)


def z_operand(count):
    high, low = two_terms(band(count))
    row = jnp.concatenate([high, low], axis=1)
    return jnp.concatenate([row, row], axis=0)


def split(value):
    high = value.astype(BF16)
    return high, (value - high.astype(F32)).astype(BF16)


def rows_of(refs, chunk, rows):
    if len(refs) == 2:
        return refs[chunk]
    return refs[0].at[:, chunk * rows : (chunk + 1) * rows]


def load_planes(sources, extended, sems, rows):
    copies = []
    for chunk in range(2):
        start, at = 0, slice(chunk * rows, (chunk + 1) * rows)
        mine = []
        for k, refs in enumerate(sources):
            source = rows_of(refs, chunk, rows)
            count = source.shape[0]
            mine.append(
                pltpu.make_async_copy(source, extended.at[start : start + count, at], sems.at[chunk * 3 + k])
            )
            start += count
        for copy in mine:
            copy.start()
        copies.append(mine)
    return copies


def x_pass(extended, copies, stacked):
    planes, rows, lanes = extended.shape
    planes -= 2 * REACH

    def step(tile, carry):
        at = pl.ds(pl.multiple_of(tile * 16, 16), 16)
        at_low = pl.ds(pl.multiple_of(tile * 16 + rows, 16), 16)
        window = [extended[i, at, :] for i in range(2 * REACH)]
        for p in range(planes):
            window.append(extended[p + 2 * REACH, at, :])
            total = TAPS[0] * window[REACH]
            for shift in range(1, REACH + 1):
                total = total + TAPS[shift] * (window[REACH - shift] + window[REACH + shift])
            window.pop(0)
            high, low = split(total)
            stacked[at, p * lanes : (p + 1) * lanes] = high
            stacked[at_low, p * lanes : (p + 1) * lanes] = low
        return carry

    tiles = rows // 16
    for chunk, mine in enumerate(copies):
        for copy in mine:
            copy.wait()
        lax.fori_loop(chunk * tiles // 2, (chunk + 1) * tiles // 2, step, 0)


def yz_plane_pair(stacked, by, bz, pair, lanes):
    rows = stacked.shape[0] // 2
    cols = pl.ds(pl.multiple_of(pair * 2 * lanes, 2 * lanes), 2 * lanes)
    both = stacked[:, cols]
    rhs = jnp.concatenate([both, both[:rows]], axis=0)
    mid = jnp.dot(by[...], rhs, preferred_element_type=F32)
    out = []
    for half in range(2):
        high, low = split(mid[:, half * lanes : (half + 1) * lanes])
        wide = jnp.dot(jnp.concatenate([high, low], axis=1), bz[...], preferred_element_type=F32)
        out.append(wide[:, :lanes] + wide[:, lanes:])
    return out


ANY = pl.BlockSpec(memory_space=pl.ANY)
SMEM = pl.BlockSpec(memory_space=pltpu.SMEM)
DMA = pltpu.SemaphoreType.DMA


def first_kernel(n_own, *refs):
    n_side = 2 if n_own == 2 else 1
    below, own, above = refs[:n_side], refs[n_side : n_side + n_own], refs[n_side + n_own : 2 * n_side + n_own]
    density, by_hbm, bz_hbm, first, low_edge, high_edge = refs[2 * n_side + n_own : 2 * n_side + n_own + 6]
    extended, logs, result, stacked, by, bz, in_sems, more_sems, out_sems = refs[2 * n_side + n_own + 6 :]
    planes, rows, lanes = result.shape
    copies = load_planes((below, own, above), extended, in_sems, rows // 2)
    more = [
        pltpu.make_async_copy(src, dst, more_sems.at[i])
        for i, (src, dst) in enumerate(((by_hbm, by), (bz_hbm, bz), (density, logs)))
    ]
    for copy in more:
        copy.start()
    x_pass(extended, copies, stacked)
    for copy in more:
        copy.wait()

    def outgoing(group):
        at = pl.ds(group * 4, 4)
        return pltpu.make_async_copy(result.at[at], first.at[at], out_sems.at[group])

    def step(group, carry):
        for inner in range(2):
            pair = group * 2 + inner
            for half, marginal in enumerate(yz_plane_pair(stacked, by, bz, pair, lanes)):
                p = pair * 2 + half
                result[p] = jnp.exp(RELAX * (logs[p] - jnp.log(marginal)))
        outgoing(group).start()
        return carry

    lax.fori_loop(0, planes // 4, step, 0)
    edges = [
        pltpu.make_async_copy(result.at[:REACH], low_edge, more_sems.at[0]),
        pltpu.make_async_copy(result.at[planes - REACH :], high_edge, more_sems.at[1]),
    ]
    for copy in edges:
        copy.start()
    for copy in edges:
        copy.wait()
    for group in range(planes // 4):
        outgoing(group).wait()


def image_kernel(n_log, places, weight, below, first, above, *refs):
    log_second = refs[:n_log]
    by_hbm, bz_hbm = refs[n_log : n_log + 2]
    pieces = refs[n_log + 2 : n_log + 10]
    log_image = refs[n_log + 10]
    extended, logs, result, part, stacked, by, bz, in_sems, more_sems, out_sems, part_sems = refs[n_log + 11 :]
    planes, rows, lanes = result.shape
    half_rows = rows // 2
    copies = load_planes(((below,), (first,), (above,)), extended, in_sems, half_rows)
    more = [pltpu.make_async_copy(by_hbm, by, more_sems.at[0]), pltpu.make_async_copy(bz_hbm, bz, more_sems.at[1])]
    for chunk in range(2):
        more.append(
            pltpu.make_async_copy(
                rows_of(log_second, chunk, half_rows),
                logs.at[:, chunk * half_rows : (chunk + 1) * half_rows],
                more_sems.at[2 + chunk],
            )
        )
    for copy in more:
        copy.start()
    x_pass(extended, copies, stacked)
    for copy in more:
        copy.wait()

    def pair_of(group, inner):
        side, which = group % 2, 1 - group // 2
        return side * (planes // 4) + ((which * 2 + inner) ^ places[side])

    def outgoing(group, inner):
        at = pl.ds(pair_of(group, inner) * 2, 2)
        return pltpu.make_async_copy(result.at[at], log_image.at[at], out_sems.at[group * 2 + inner])

    def piece_copy(group, chunk):
        return pltpu.make_async_copy(
            part.at[group * 4 : group * 4 + 4, chunk * half_rows : (chunk + 1) * half_rows],
            pieces[group * 2 + chunk],
            part_sems.at[group * 2 + chunk],
        )

    def step(group, carry):
        for inner in range(2):
            pair = pair_of(group, inner)
            for half, image in enumerate(yz_plane_pair(stacked, by, bz, pair, lanes)):
                p = pair * 2 + half
                new = jnp.log(image)
                result[p] = new
                part[group * 4 + inner * 2 + half] = weight[0] * (logs[p] + new)
            outgoing(group, inner).start()
        for g in range(4):

            @pl.when(group == g)
            def _():
                for chunk in range(2):
                    piece_copy(g, chunk).start()

        return carry

    lax.fori_loop(0, 4, step, 0)
    for g in range(4):
        for k in range(2):
            outgoing(g, k).wait()
            piece_copy(g, k).wait()


def second_kernel(chunk, last, places, keep_a, more_a, keep_b, more_b, log_image, *refs):
    if last and chunk == 1:
        refs = refs[2:]
    outs = refs[: 2 if last else 4]
    incoming, images, second_buf, other_buf, piece_sems, out_sems = refs[2 if last else 4 :]
    planes, rows, lanes = second_buf.shape
    arrivals = [pltpu.make_async_copy(log_image.at[:, chunk * rows : (chunk + 1) * rows], images, out_sems.at[0])]
    for k, piece in enumerate((keep_a, keep_b, more_a, more_b)):
        arrivals.append(pltpu.make_async_copy(piece, incoming.at[k], piece_sems.at[k]))
    for copy in arrivals:
        copy.start()
    arrivals[0].wait()
    for k, copy in enumerate(arrivals[1:]):
        copy.wait()
        side, which = k % 2, k // 2

        def step(tile, carry):
            inner, at = tile // (rows // 32), pl.ds(pl.multiple_of((tile % (rows // 32)) * 32, 32), 32)
            pair = side * (planes // 4) + ((which * 2 + inner) ^ places[side])
            for half in range(2):
                logmean = incoming[k, inner * 2 + half, at, :]
                p = pair * 2 + half
                logs = RELAX * (logmean - images[p, at, :])
                second_buf[p, at, :] = jnp.exp(logs)
                other_buf[p, at, :] = jnp.exp(logmean) if last else logs
            return carry

        lax.fori_loop(0, 2 * (rows // 32), step, 0)
    if last:
        at = slice(chunk * rows, (chunk + 1) * rows)
        routes = ((second_buf, outs[0].at[:, at]), (other_buf, outs[1].at[:, at]))
    else:
        routes = (
            (second_buf.at[:REACH], outs[2]),
            (second_buf.at[planes - REACH :], outs[3]),
            (second_buf, outs[0]),
            (other_buf, outs[1]),
        )
    leaving = [pltpu.make_async_copy(src, dst, out_sems.at[i]) for i, (src, dst) in enumerate(routes)]
    for copy in leaving:
        copy.start()
    for copy in leaving:
        copy.wait()


def body(density, scaling, weights):
    planes, rows, lanes = density.shape[1:]
    half_rows = rows // 2
    shape = lambda p, r: jax.ShapeDtypeStruct((p, r, lanes), F32)
    cube, slab = shape(planes, rows), shape(planes, half_rows)
    buffer = lambda p, r: pltpu.VMEM((p, r, lanes), F32)
    by, bz = y_operand(rows), z_operand(lanes)
    count = lax.axis_size("space")
    spot = lax.axis_index("embryo")
    x = spot % 4
    mix, top = (x & 1) ^ (x >> 1), x >> 1
    places = jnp.stack([mix * 2 + top, top * 2 + mix]).astype(jnp.int32)
    weight = (weights / jnp.sum(weights))[spot][None]

    cells = planes * rows * lanes
    cost = pl.CostEstimate(flops=cells * 3000, bytes_accessed=cells * 16, transcendentals=cells * 2)
    small_cost = pl.CostEstimate(flops=cells * 4, bytes_accessed=cells * 8, transcendentals=cells)
    shared = [
        pltpu.VMEM((2 * rows, planes * lanes), BF16),
        pltpu.VMEM(by.shape, BF16),
        pltpu.VMEM(bz.shape, BF16),
        DMA((6,)),
        DMA((4,)),
        DMA((8,)),
    ]

    def first_call(below, own, above):
        return pl.pallas_call(
            lambda *refs: first_kernel(len(own), *refs),
            out_shape=(cube, shape(REACH, rows), shape(REACH, rows)),
            in_specs=[ANY] * (len(below) + len(own) + len(above) + 3),
            out_specs=(ANY,) * 3,
            scratch_shapes=[buffer(planes + 2 * REACH, rows), buffer(planes, rows), buffer(planes, rows)] + shared,
            cost_estimate=cost,
            name="first",
        )(*below, *own, *above, log_density, by, bz)

    def image_call(below, first, above, log_second):
        *pieces, log_image = pl.pallas_call(
            lambda *refs: image_kernel(len(log_second), *refs),
            out_shape=(shape(planes // 4, half_rows),) * 8 + (cube,),
            in_specs=[SMEM, SMEM] + [ANY] * (len(log_second) + 5),
            out_specs=(ANY,) * 9,
            scratch_shapes=[buffer(planes + 2 * REACH, rows)] + [buffer(planes, rows)] * 3 + shared + [DMA((8,))],
            cost_estimate=cost,
            name="image",
        )(places, weight, below, first, above, *log_second, by, bz)
        return pieces, log_image

    def second_call(chunk, last, pieces, log_image, *so_far):
        quarter = planes // 4
        return pl.pallas_call(
            lambda *refs: second_kernel(chunk, last, *refs),
            out_shape=(cube, cube) if last else (slab, slab) + (shape(REACH, half_rows),) * 2,
            in_specs=[SMEM] + [ANY] * (5 + len(so_far)),
            out_specs=(ANY,) * (2 if last else 4),
            scratch_shapes=[pltpu.VMEM((4, quarter, half_rows, lanes), F32)]
            + [buffer(planes, half_rows)] * 3
            + [DMA((4,)), DMA((4,))],
            input_output_aliases={6 + i: i for i in range(len(so_far))},
            cost_estimate=small_cost,
            name="last" if last else "second",
        )(places, *pieces, log_image, *so_far)

    up = [(i, i + 1) for i in range(count - 1)]
    down = [(i + 1, i) for i in range(count - 1)]

    def halo(low_edge, high_edge):
        return lax.ppermute(high_edge, "space", up), lax.ppermute(low_edge, "space", down)

    def partner_x(mask):
        return [(z * 4 + i, z * 4 + (i ^ mask)) for z in range(4) for i in range(4)]

    def partner_z(mask):
        return [(z * 4 + i, (z ^ mask) * 4 + i) for z in range(4) for i in range(4)]

    near, wrap = (partner_x(1), partner_x(3)), (partner_x(3), partner_x(1))
    z_near, z_wrap = (partner_z(1), partner_z(3)), (partner_z(3), partner_z(1))

    def swap(values, perms):
        values = lax.optimization_barrier(values)
        return lax.optimization_barrier([lax.ppermute(v, "embryo", p) for v, p in zip(values, perms)])

    def all_sum(give, keep):
        held = [k + g for k, g in zip(keep, swap(give, near))]
        mid = planes // 8
        got = swap([v[mid:] for v in held], wrap)
        held = [v[:mid] + g for v, g in zip(held, got)]
        held = [v + g for v, g in zip(held, swap(held, z_near))]
        held = [v + g for v, g in zip(held, swap(held, z_wrap))]
        held = [jnp.concatenate([v, g], axis=0) for v, g in zip(held, swap(held, wrap))]
        more = swap(held, near)
        return held[0], more[0], held[1], more[1]

    second = (scaling[0],)
    below, above = halo(scaling[0, :REACH], scaling[0, planes - REACH :])
    below, above = (below,), (above,)
    log_density = jnp.log(density[0])
    log_second = (jnp.log(scaling[0]),)
    for sweep in range(ITERS):
        first, low_edge, high_edge = first_call(below, second, above)
        below, above = halo(low_edge, high_edge)
        pieces, log_image = image_call(below, first, above, log_second)
        summed = [all_sum((pieces[c], pieces[2 + c]), (pieces[4 + c], pieces[6 + c])) for c in range(2)]
        if sweep == ITERS - 1:
            so_far = second_call(0, True, summed[0], log_image)
            second, mean = second_call(1, True, summed[1], log_image, *so_far)
            break
        second, log_second, below, above = [], [], [], []
        for chunk in range(2):
            new, logs, low_edge, high_edge = second_call(chunk, False, summed[chunk], log_image)
            low, high = halo(low_edge, high_edge)
            second.append(new)
            log_second.append(logs)
            below.append(low)
            above.append(high)
    return mean, first[None], second[None]


def solution(mesh):
    return jax.shard_map(
        body,
        mesh=mesh,
        in_specs=(P("embryo", "space", None, None), P("embryo", "space", None, None), P()),
        out_specs=(
            P("space", None, None),
            P("embryo", "space", None, None),
            P("embryo", "space", None, None),
        ),
        check_vma=False,
    )
```

```python
import math

import jax
import jax.numpy as jnp
import numpy as np
from jax import lax
from jax.experimental import pallas as pl
from jax.experimental.pallas import tpu as pltpu
from jax.sharding import PartitionSpec as P

ITERS = 3
RELAX = 0.8
REACH = 6
BF16 = jnp.bfloat16
F32 = jnp.float32


def tap_values():
    raw = np.exp(-np.arange(-REACH, REACH + 1, dtype=np.float64) ** 2 / 18.0)
    return raw / raw.sum()


TAPS = [float(v) for v in tap_values()[REACH:]]


def band(count):
    away = np.abs(np.arange(count)[:, None] - np.arange(count)[None, :])
    full = np.zeros((count, count))
    taps = tap_values()
    for shift in range(REACH + 1):
        full[away == shift] = taps[REACH + shift]
    return full.astype(np.float32)


def two_terms(matrix):
    high = jnp.asarray(matrix).astype(BF16)
    low = (jnp.asarray(matrix) - high.astype(F32)).astype(BF16)
    return high, low


def y_operand(count):
    high, low = two_terms(band(count))
    return jnp.concatenate([high, high, low], axis=1)


def z_operand(count):
    high, low = two_terms(band(count))
    row = jnp.concatenate([high, low], axis=1)
    return jnp.concatenate([row, row], axis=0)


def split(value):
    high = value.astype(BF16)
    return high, (value - high.astype(F32)).astype(BF16)


def x_pass(extended, copies, stacked):
    planes, rows, lanes = extended.shape
    planes -= 2 * REACH

    def step(tile, carry):
        at = pl.ds(pl.multiple_of(tile * 16, 16), 16)
        at_low = pl.ds(pl.multiple_of(tile * 16 + rows, 16), 16)
        window = [extended[i, at, :] for i in range(2 * REACH)]
        for p in range(planes):
            window.append(extended[p + 2 * REACH, at, :])
            total = TAPS[0] * window[REACH]
            for shift in range(1, REACH + 1):
                total = total + TAPS[shift] * (window[REACH - shift] + window[REACH + shift])
            window.pop(0)
            high, low = split(total)
            stacked[at, p * lanes : (p + 1) * lanes] = high
            stacked[at_low, p * lanes : (p + 1) * lanes] = low
        return carry

    tiles = rows // 16
    for part, mine in enumerate(copies):
        for copy in mine:
            copy.wait()
        lax.fori_loop(part * tiles // 2, (part + 1) * tiles // 2, step, 0)


def yz_plane_pair(stacked, by, bz, pair, lanes):
    rows = stacked.shape[0] // 2
    cols = pl.ds(pl.multiple_of(pair * 2 * lanes, 2 * lanes), 2 * lanes)
    both = stacked[:, cols]
    rhs = jnp.concatenate([both, both[:rows]], axis=0)
    mid = jnp.dot(by[...], rhs, preferred_element_type=F32)
    out = []
    for half in range(2):
        high, low = split(mid[:, half * lanes : (half + 1) * lanes])
        wide = jnp.dot(jnp.concatenate([high, low], axis=1), bz[...], preferred_element_type=F32)
        out.append(wide[:, :lanes] + wide[:, lanes:])
    return out


ANY = pl.BlockSpec(memory_space=pl.ANY)
SMEM = pl.BlockSpec(memory_space=pltpu.SMEM)
DMA = pltpu.SemaphoreType.DMA
GRANT = 20 << 20


def first_kernel(core, got_far, own, got_near, density, by_hbm, bz_hbm, first, edge_far, edge_near, *scratch):
    extended, logs, result, stacked, by, bz, in_sems, more_sems, out_sems = scratch
    planes, rows, lanes = result.shape
    far_end, near_end = core[0], 1 - core[0]
    copies = []
    for part in range(2):
        at = slice(part * rows // 2, (part + 1) * rows // 2)
        mine = []
        for k, (source, start) in enumerate(
            ((got_far, far_end * (planes + REACH)), (own, REACH), (got_near, near_end * (planes + REACH)))
        ):
            mine.append(
                pltpu.make_async_copy(
                    source.at[:, at], extended.at[pl.ds(start, source.shape[0]), at], in_sems.at[part * 3 + k]
                )
            )
        for copy in mine:
            copy.start()
        copies.append(mine)
    more = [
        pltpu.make_async_copy(src, dst, more_sems.at[i])
        for i, (src, dst) in enumerate(((by_hbm, by), (bz_hbm, bz), (density, logs)))
    ]
    for copy in more:
        copy.start()
    x_pass(extended, copies, stacked)
    for copy in more:
        copy.wait()

    def outgoing(group):
        at = pl.ds(group * 4, 4)
        return pltpu.make_async_copy(result.at[at], first.at[at], out_sems.at[group])

    def step(group, carry):
        for inner in range(2):
            pair = group * 2 + inner
            for half, marginal in enumerate(yz_plane_pair(stacked, by, bz, pair, lanes)):
                p = pair * 2 + half
                result[p] = jnp.exp(RELAX * (logs[p] - jnp.log(marginal)))
        outgoing(group).start()
        return carry

    lax.fori_loop(0, planes // 4, step, 0)
    send_edges(result, far_end, near_end, edge_far, edge_near, more_sems)
    for group in range(planes // 4):
        outgoing(group).wait()


def send_edges(result, far_end, near_end, edge_far, edge_near, sems):
    inside = result.shape[0] - REACH
    edges = [
        pltpu.make_async_copy(result.at[pl.ds(far_end * inside, REACH)], edge_far, sems.at[0]),
        pltpu.make_async_copy(result.at[pl.ds(near_end * inside, REACH)], edge_near, sems.at[1]),
    ]
    for copy in edges:
        copy.start()
    for copy in edges:
        copy.wait()


def image_kernel(chunk, core, places, weight, got_far, first, got_near, second, by_hbm, bz_hbm, *refs):
    pieces, log_image = refs[:4], refs[4]
    extended, logs, result, part, stacked, by, bz, in_sems, more_sems, out_sems = refs[5:]
    planes, rows, lanes = result.shape
    span = planes + REACH
    own_at, halo_at, own_from = (REACH, 0, 0) if chunk == 0 else (0, span, first.shape[0] - span)
    copies = []
    for half in range(2):
        at = slice(half * rows // 2, (half + 1) * rows // 2)
        own = pltpu.make_async_copy(
            first.at[own_from : own_from + span, at], extended.at[own_at : own_at + span, at], in_sems.at[half * 2]
        )
        own.start()
        side = [
            pltpu.make_async_copy(
                got.at[:, at], extended.at[halo_at : halo_at + REACH, at], in_sems.at[half * 2 + 1]
            )
            for got in (got_far, got_near)
        ]

        @pl.when(core[0] == chunk)
        def _():
            side[0].start()

        @pl.when(core[0] != chunk)
        def _():
            side[1].start()

        copies.append([own, side[0]])
    more = [
        pltpu.make_async_copy(src, dst, more_sems.at[i])
        for i, (src, dst) in enumerate(
            ((by_hbm, by), (bz_hbm, bz), (second.at[chunk * planes : (chunk + 1) * planes], logs))
        )
    ]
    for copy in more:
        copy.start()
    x_pass(extended, copies, stacked)
    for copy in more:
        copy.wait()
    quarter = planes // 4

    def outgoing(side):
        at = pl.ds(side * 2 * quarter, 2 * quarter)
        return pltpu.make_async_copy(result.at[at], log_image.at[at], out_sems.at[side])

    def piece_copy(k):
        return pltpu.make_async_copy(part.at[k * quarter : (k + 1) * quarter], pieces[k], out_sems.at[2 + k])

    def step(side, carry):
        for inner in range(2):
            pair = side * 2 + inner
            for half, image in enumerate(yz_plane_pair(stacked, by, bz, pair, lanes)):
                p = pair * 2 + half
                new = jnp.log(image)
                result[p] = new
                slot = side * 4 + ((inner * 2 + half) ^ places[side])
                part[slot] = weight[0] * (jnp.log(logs[p]) + new)
        outgoing(side).start()
        for s in range(2):

            @pl.when(side == s)
            def _():
                piece_copy(s * 2).start()
                piece_copy(s * 2 + 1).start()

        return carry

    lax.fori_loop(0, 2, step, 0)
    for k in range(4):
        piece_copy(k).wait()
    for side in range(2):
        outgoing(side).wait()


def second_kernel(last, core, places, *refs):
    pieces, log_images, refs = refs[:8], refs[8:10], refs[10:]
    outs, refs = refs[: 2 if last else 3], refs[2 if last else 3 :]
    incoming, images, second_buf, mean_buf, piece_sems, out_sems = refs
    planes, rows, lanes = second_buf.shape
    half = planes // 2
    arrivals = []
    for chunk in range(2):
        copy = pltpu.make_async_copy(
            log_images[chunk], images.at[chunk * half : (chunk + 1) * half], out_sems.at[chunk]
        )
        copy.start()
        arrivals.append(copy)
    landing = [pltpu.make_async_copy(piece, incoming.at[k], piece_sems.at[k]) for k, piece in enumerate(pieces)]
    for copy in landing:
        copy.start()
    for copy in arrivals:
        copy.wait()
    leaving = []
    for k, copy in enumerate(landing):
        copy.wait()
        chunk, side, which = k // 4, k % 4 // 2, k % 2
        for i in range(2):
            p = chunk * half + side * 4 + ((which * 2 + i) ^ places[side])

            def step(tile, carry):
                at = pl.ds(pl.multiple_of(tile * 128, 128), 128)
                logmean = incoming[k, i, at, :]
                second_buf[p, at, :] = jnp.exp(RELAX * (logmean - images[p, at, :]))
                if last:
                    mean_buf[p, at, :] = jnp.exp(logmean)
                return carry

            lax.fori_loop(0, rows // 128, step, 0)
            out = [pltpu.make_async_copy(second_buf.at[p], outs[0].at[p], out_sems.at[2 + k * 4 + i])]
            if last:
                out.append(pltpu.make_async_copy(mean_buf.at[p], outs[1].at[p], out_sems.at[2 + k * 4 + 2 + i]))
            for copy_out in out:
                copy_out.start()
            leaving += out
    if not last:
        send_edges(second_buf, core[0], 1 - core[0], outs[1], outs[2], piece_sems)
    for copy in leaving:
        copy.wait()


def body(density, scaling, weights):
    planes, rows, lanes = density.shape[1:]
    half = planes // 2
    shape = lambda p: jax.ShapeDtypeStruct((p, rows, lanes), F32)
    buffer = lambda p: pltpu.VMEM((p, rows, lanes), F32)
    by, bz = y_operand(rows), z_operand(lanes)
    count = lax.axis_size("space")
    core = (lax.axis_index("space") % 2).astype(jnp.int32)
    spot = lax.axis_index("embryo")
    x = spot % 4
    mix, top = (x & 1) ^ (x >> 1), x >> 1
    places = jnp.stack([mix * 2 + top, top * 2 + mix]).astype(jnp.int32)
    weight = (weights / jnp.sum(weights))[spot][None]
    params = pltpu.CompilerParams(vmem_limit_bytes=GRANT)

    cells = planes * rows * lanes
    cost = pl.CostEstimate(flops=cells * 3000, bytes_accessed=cells * 16, transcendentals=cells * 2)
    half_cost = pl.CostEstimate(flops=cells * 1500, bytes_accessed=cells * 8, transcendentals=cells)
    small_cost = pl.CostEstimate(flops=cells * 4, bytes_accessed=cells * 12, transcendentals=cells)

    def constants(p):
        return [pltpu.VMEM((2 * rows, p * lanes), BF16), pltpu.VMEM(by.shape, BF16), pltpu.VMEM(bz.shape, BF16)]

    def first_call(far, own, near):
        return pl.pallas_call(
            first_kernel,
            out_shape=(shape(planes), shape(REACH), shape(REACH)),
            in_specs=[SMEM] + [ANY] * 6,
            out_specs=(ANY,) * 3,
            scratch_shapes=[buffer(planes + 2 * REACH), buffer(planes), buffer(planes)]
            + constants(planes)
            + [DMA((6,)), DMA((3,)), DMA((4,))],
            compiler_params=params,
            cost_estimate=cost,
            name="first",
        )(core[None], far, own, near, log_density, by, bz)

    def image_call(chunk, far, first, near, second):
        *pieces, log_image = pl.pallas_call(
            lambda *refs: image_kernel(chunk, *refs),
            out_shape=(shape(half // 4),) * 4 + (shape(half),),
            in_specs=[SMEM] * 3 + [ANY] * 6,
            out_specs=(ANY,) * 5,
            scratch_shapes=[buffer(half + 2 * REACH)]
            + [buffer(half)] * 3
            + constants(half)
            + [DMA((4,)), DMA((3,)), DMA((6,))],
            compiler_params=params,
            cost_estimate=half_cost,
            name="image",
        )(core[None], places, weight, far, first, near, second, by, bz)
        return pieces, log_image

    def second_call(last, pieces, log_images):
        return pl.pallas_call(
            lambda *refs: second_kernel(last, *refs),
            out_shape=(shape(planes), shape(planes)) if last else (shape(planes), shape(REACH), shape(REACH)),
            in_specs=[SMEM] * 2 + [ANY] * 10,
            out_specs=(ANY,) * (2 if last else 3),
            scratch_shapes=[pltpu.VMEM((8, planes // 8, rows, lanes), F32)]
            + [buffer(planes)] * 3
            + [DMA((8,)), DMA((34,))],
            compiler_params=params,
            cost_estimate=small_cost,
            name="last" if last else "second",
        )(core[None], places, *pieces, *log_images)

    far_pairs = [(i, i + 1) for i in range(1, count - 1, 2)]
    near_pairs = [(i, i + 1) for i in range(0, count, 2)]
    both_ways = lambda pairs: pairs + [(b, a) for a, b in pairs]

    def halo(edge_far, edge_near):
        return (
            lax.ppermute(edge_far, "space", both_ways(far_pairs)),
            lax.ppermute(edge_near, "space", both_ways(near_pairs)),
        )

    def partner_x(mask):
        return [(z * 4 + i, z * 4 + (i ^ mask)) for z in range(4) for i in range(4)]

    def partner_z(mask):
        return [(z * 4 + i, (z ^ mask) * 4 + i) for z in range(4) for i in range(4)]

    near_x, wrap_x = (partner_x(1), partner_x(3)), (partner_x(3), partner_x(1))
    near_z, wrap_z = (partner_z(1), partner_z(3)), (partner_z(3), partner_z(1))

    def swap(values, perms):
        values = lax.optimization_barrier(values)
        return lax.optimization_barrier([lax.ppermute(v, "embryo", p) for v, p in zip(values, perms)])

    def all_sum(pieces):
        held = [k + g for k, g in zip(pieces[0::2], swap(pieces[1::2], near_x))]
        mid = held[0].shape[0] // 2
        got = swap([v[mid:] for v in held], wrap_x)
        held = [v[:mid] + g for v, g in zip(held, got)]
        held = [v + g for v, g in zip(held, swap(held, near_z))]
        held = [v + g for v, g in zip(held, swap(held, wrap_z))]
        held = [jnp.concatenate([v, g], axis=0) for v, g in zip(held, swap(held, wrap_x))]
        more = swap(held, near_x)
        return held[0], more[0], held[1], more[1]

    second = scaling[0]
    inside = planes - REACH
    edges = [lax.dynamic_slice_in_dim(second, end * inside, REACH, axis=0) for end in (core, 1 - core)]
    log_density = jnp.log(density[0])
    for sweep in range(ITERS):
        far, near = halo(*edges)
        first, *edges = first_call(far, second, near)
        far, near = halo(*edges)
        summed, log_images = [], []
        for chunk in range(2):
            pieces, log_image = image_call(chunk, far, first, near, second)
            summed += all_sum(pieces)
            log_images.append(log_image)
        second, *edges = second_call(sweep == ITERS - 1, summed, log_images)
    return edges[0], first[None], second[None]


def solution(mesh):
    return jax.shard_map(
        body,
        mesh=mesh,
        in_specs=(P("embryo", "space", None, None), P("embryo", "space", None, None), P()),
        out_specs=(
            P("space", None, None),
            P("embryo", "space", None, None),
            P("embryo", "space", None, None),
        ),
        check_vma=False,
    )
```

```python
import jax
import jax.numpy as jnp
import numpy as np
from jax import lax
from jax.experimental import pallas as pl
from jax.experimental.pallas import tpu as pltpu
from jax.sharding import PartitionSpec as P


ITERS = 3
RELAX = 0.8
REACH = 6
BF16 = jnp.bfloat16
F32 = jnp.float32


def tap_values():
    raw = np.exp(-np.arange(-REACH, REACH + 1, dtype=np.float64) ** 2 / 18.0)
    return raw / raw.sum()


TAPS = [float(v) for v in tap_values()[REACH:]]


def band(count):
    away = np.abs(np.arange(count)[:, None] - np.arange(count)[None, :])
    full = np.zeros((count, count))
    taps = tap_values()
    for shift in range(REACH + 1):
        full[away == shift] = taps[REACH + shift]
    return full.astype(np.float32)


def two_terms(matrix):
    high = jnp.asarray(matrix).astype(BF16)
    low = (jnp.asarray(matrix) - high.astype(F32)).astype(BF16)
    return high, low


def y_operand(count):
    high, low = two_terms(band(count))
    return jnp.concatenate([high, high, low], axis=1)


def z_operand(count):
    high, low = two_terms(band(count))
    row = jnp.concatenate([high, low], axis=1)
    return jnp.concatenate([row, row], axis=0)


def split(value):
    high = value.astype(BF16)
    return high, (value - high.astype(F32)).astype(BF16)


def x_pass(sources, stacked, rows, lanes):
    planes = len(sources) - 2 * REACH

    def step(tile, carry):
        at = pl.ds(pl.multiple_of(tile * 16, 16), 16)
        at_low = pl.ds(pl.multiple_of(tile * 16 + rows, 16), 16)
        load = lambda i: sources[i][0][sources[i][1], at, :]
        window = [load(i) for i in range(2 * REACH)]
        for p in range(planes):
            window.append(load(p + 2 * REACH))
            total = TAPS[0] * window[REACH]
            for shift in range(1, REACH + 1):
                total = total + TAPS[shift] * (window[REACH - shift] + window[REACH + shift])
            window.pop(0)
            high, low = split(total)
            stacked[at, p * lanes : (p + 1) * lanes] = high
            stacked[at_low, p * lanes : (p + 1) * lanes] = low
        return carry

    lax.fori_loop(0, rows // 16, step, 0)


def yz_plane_pair(stacked, by, bz, pair, lanes):
    rows = stacked.shape[0] // 2
    both = stacked[:, pair * 2 * lanes : (pair + 1) * 2 * lanes]
    rhs = jnp.concatenate([both, both[:rows]], axis=0)
    mid = jnp.dot(by[...], rhs, preferred_element_type=F32)
    out = []
    for half in range(2):
        high, low = split(mid[:, half * lanes : (half + 1) * lanes])
        wide = jnp.dot(jnp.concatenate([high, low], axis=1), bz[...], preferred_element_type=F32)
        out.append(wide[:, :lanes] + wide[:, lanes:])
    return out


ANY = pl.BlockSpec(memory_space=pl.ANY)
SMEM = pl.BlockSpec(memory_space=pltpu.SMEM)
VMEM = pl.BlockSpec(memory_space=pltpu.VMEM)
DMA = pltpu.SemaphoreType.DMA
GRANT = 12 << 20


def around(center, other, halo):
    mirrored = [(halo, REACH - 1 - i) for i in range(REACH)]
    own = [(center, i) for i in range(center.shape[0])]
    inner = [(other, i) for i in range(REACH)]
    if center.shape[0] == REACH:
        return mirrored + own + inner
    return inner + own + mirrored


def first_kernel(center, other, halo, log_density, by, bz, first, *rest):
    edge, stacked = rest[:-1], rest[-1]
    count, rows, lanes = center.shape
    x_pass(around(center, other, halo), stacked, rows, lanes)
    for pair in range(count // 2):
        for half, marginal in enumerate(yz_plane_pair(stacked, by, bz, pair, lanes)):
            p = pair * 2 + half
            value = jnp.exp(RELAX * (log_density[p] - jnp.log(marginal)))
            first[p] = value
            if edge and p >= count - REACH:
                edge[0][p - count + REACH] = value


def image_kernel(places, weight, center, other, halo, second, by, bz, *refs):
    pieces, log_image, stacked = refs[:4], refs[4], refs[5]
    count, rows, lanes = center.shape
    x_pass(around(center, other, halo), stacked, rows, lanes)
    side_count, quarter = count // 2, rows // 4
    for pair in range(count // 2):
        for half, image in enumerate(yz_plane_pair(stacked, by, bz, pair, lanes)):
            log_image[pair * 2 + half] = jnp.log(image)
        for half in range(2):
            p = pair * 2 + half
            side = p // side_count
            for slot in range(4):
                at = pl.ds(pl.multiple_of((slot ^ places[side]) * quarter, quarter), quarter)
                out = slice((slot % 2) * quarter, (slot % 2 + 1) * quarter)
                value = weight[0] * (jnp.log(second[p, at, :]) + log_image[p, at, :])
                pieces[side * 2 + slot // 2][p - side * side_count, out, :] = value


def second_kernel(last, places, *refs):
    pieces, log_image, second, extra = refs[:4], refs[4], refs[5], refs[6:]
    count, rows, _ = second.shape
    side_count, quarter = count // 2, rows // 4
    for k, piece in enumerate(pieces):
        side, which = k // 2, k % 2
        for i in range(side_count):
            p = side * side_count + i
            for b in range(2):
                at = pl.ds(pl.multiple_of(((which * 2 + b) ^ places[side]) * quarter, quarter), quarter)
                logmean = piece[i, b * quarter : (b + 1) * quarter, :]
                value = jnp.exp(RELAX * (logmean - log_image[p, at, :]))
                second[p, at, :] = value
                if last:
                    extra[0][p, at, :] = jnp.exp(logmean)
                elif extra and p >= count - REACH:
                    extra[0][p - count + REACH, at, :] = value


def placed(core, d, planes):
    return core[0] * (planes - 1 - d) + (1 - core[0]) * d


def split_kernel(logs, core, whole, *outs):
    planes = whole.shape[0]
    for out, low in zip(outs, (REACH, 0, planes - REACH)):

        def step(i, carry):
            cells = whole[placed(core, low + i, planes)]
            out[i] = jnp.log(cells) if logs else cells
            return carry

        lax.fori_loop(0, out.shape[0], step, 0)


def join_kernel(core, *refs):
    sems = refs[-1]
    n = (len(refs) - 1) // 3
    parts, wholes = refs[: 2 * n], refs[2 * n : 3 * n]
    planes = wholes[0].shape[0]
    copies = []
    for k, whole in enumerate(wholes):
        for part, low in zip(parts[2 * k : 2 * k + 2], (REACH, 0)):
            for i in range(part.shape[0]):
                target = whole.at[placed(core, low + i, planes)]
                copies.append(pltpu.make_async_copy(part.at[i], target, sems.at[k, low + i]))
                copies[-1].start()
    for copy in copies:
        copy.wait()


def body(density, scaling, weights):
    density, scaling = density[0], scaling[0]
    planes, rows, lanes = density.shape
    shape = lambda p, r=rows: jax.ShapeDtypeStruct((p, r, lanes), F32)
    main_count = planes - REACH
    by, bz = y_operand(rows), z_operand(lanes)
    count = lax.axis_size("space")
    core = (lax.axis_index("space") % 2).astype(jnp.int32)[None]
    spot = lax.axis_index("embryo")
    x = spot % 4
    mix, top = (x & 1) ^ (x >> 1), x >> 1
    places = jnp.stack([mix * 2 + top, top * 2 + mix]).astype(jnp.int32)
    weight = (weights / jnp.sum(weights))[spot][None]
    params = pltpu.CompilerParams(vmem_limit_bytes=GRANT)

    def cost(p, flops, passes, exps):
        cells = p * rows * lanes
        return pl.CostEstimate(flops=cells * flops, bytes_accessed=cells * 4 * passes, transcendentals=cells * exps)

    def stacked(p):
        return [pltpu.VMEM((2 * rows, p * lanes), BF16)]

    def first_call(center, other, halo, log_density):
        p = center.shape[0]
        edge = (shape(REACH),) if p != REACH else ()
        return pl.pallas_call(
            first_kernel,
            out_shape=(shape(p),) + edge,
            in_specs=[VMEM] * 6,
            out_specs=(VMEM,) * (1 + len(edge)),
            scratch_shapes=stacked(p),
            compiler_params=params,
            cost_estimate=cost(p, 3000, 4, 3),
            name="first",
        )(center, other, halo, log_density, by, bz)

    def image_call(center, other, halo, second):
        p = center.shape[0]
        *pieces, log_image = pl.pallas_call(
            image_kernel,
            out_shape=(shape(p // 2, rows // 2),) * 4 + (shape(p),),
            in_specs=[SMEM] * 2 + [VMEM] * 6,
            out_specs=(VMEM,) * 5,
            scratch_shapes=stacked(p),
            compiler_params=params,
            cost_estimate=cost(p, 3000, 4, 3),
            name="image",
        )(places, weight, center, other, halo, second, by, bz)
        return pieces, log_image

    def second_call(last, held, more, log_image):
        p = log_image.shape[0]
        extra = (shape(p),) if last else (shape(REACH),) if p != REACH else ()
        return pl.pallas_call(
            lambda *refs: second_kernel(last, *refs),
            out_shape=(shape(p),) + extra,
            in_specs=[SMEM] + [VMEM] * 5,
            out_specs=(VMEM,) * (1 + len(extra)),
            compiler_params=params,
            cost_estimate=cost(p, 4, 3, 1),
            name="last" if last else "second",
        )(places, held[0], more[0], held[1], more[1], log_image)

    def split_call(logs, whole):
        outs = (shape(main_count), shape(REACH)) + (() if logs else (shape(REACH),))
        return pl.pallas_call(
            lambda *refs: split_kernel(logs, *refs),
            out_shape=outs,
            in_specs=[SMEM, VMEM],
            out_specs=(VMEM,) * len(outs),
            compiler_params=params,
            cost_estimate=cost(planes, 1, 2, 1),
            name="split",
        )(core, whole)

    def join_call(*parts):
        n = len(parts) // 2
        return pl.pallas_call(
            join_kernel,
            out_shape=(shape(planes),) * n,
            in_specs=[SMEM] + [VMEM] * len(parts),
            out_specs=(ANY,) * n,
            scratch_shapes=[DMA((n, planes))],
            compiler_params=params,
            cost_estimate=cost(planes, 1, 2 * n, 0),
            name="join",
        )(core, *parts)

    far_pairs = [(i, i + 1) for i in range(1, count - 1, 2)]
    near_pairs = [(i, i + 1) for i in range(0, count, 2)]

    def trade(value, pairs):
        return lax.ppermute(value, "space", pairs + [(b, a) for a, b in pairs])

    def partner_x(mask):
        return [(z * 4 + i, z * 4 + (i ^ mask)) for z in range(4) for i in range(4)]

    def partner_z(mask):
        return [(z * 4 + i, (z ^ mask) * 4 + i) for z in range(4) for i in range(4)]

    near_x, wrap_x = (partner_x(1), partner_x(3)), (partner_x(3), partner_x(1))
    near_z, wrap_z = (partner_z(1), partner_z(3)), (partner_z(3), partner_z(1))

    def swap(values, perms):
        values = lax.optimization_barrier(values)
        return lax.optimization_barrier([lax.ppermute(v, "embryo", p) for v, p in zip(values, perms)])

    def rest_of_sum(pieces, got):
        held = [k + g for k, g in zip(pieces[0::2], got)]
        mid = held[0].shape[1] // 2
        got = swap([v[:, mid:] for v in held], wrap_x)
        held = [v[:, :mid] + g for v, g in zip(held, got)]
        held = [v + g for v, g in zip(held, swap(held, near_z))]
        held = [v + g for v, g in zip(held, swap(held, wrap_z))]
        got = swap(held, wrap_x)
        held = [jnp.concatenate([v, g], axis=1) for v, g in zip(held, got)]
        return held, swap(held, near_x)

    def sweep(state, split_density, last):
        second_main, second_far, edge, density_parts = state
        far = trade(second_far, far_pairs)
        near = trade(edge, near_pairs)
        if split_density:
            density_parts = split_call(True, density)
        density_main, density_far = density_parts
        first_main, edge = first_call(second_main, second_far, near, density_main)
        near = trade(edge, near_pairs)
        (first_far,) = first_call(second_far, second_main, far, density_far)
        far = trade(first_far, far_pairs)
        pieces_main, log_main = image_call(first_main, first_far, near, second_main)
        got_main = swap(pieces_main[1::2], near_x)
        pieces_far, log_far = image_call(first_far, first_main, far, second_far)
        got_main, pieces_far = lax.optimization_barrier((got_main, pieces_far))
        got_far = swap(pieces_far[1::2], near_x)
        held_main, more_main = rest_of_sum(pieces_main, got_main)
        held_far, more_far = rest_of_sum(pieces_far, got_far)
        more_main, more_far = lax.optimization_barrier((more_main, more_far))
        second_far, *extra_far = second_call(last, held_far, more_far, log_far)
        second_main, *extra = second_call(last, held_main, more_main, log_main)
        return (second_main, second_far, extra[0], density_parts), extra_far, (first_main, first_far)

    state = (*split_call(False, scaling), None)
    for index in range(ITERS):
        state, extra_far, first_parts = sweep(state, index == 0, index == ITERS - 1)
    second_main, second_far, mean_main, _ = state
    (first,) = join_call(*first_parts)
    second, mean = join_call(second_main, second_far, mean_main, *extra_far)
    return mean, first[None], second[None]


def solution(mesh):
    return jax.shard_map(
        body,
        mesh=mesh,
        in_specs=(P("embryo", "space", None, None), P("embryo", "space", None, None), P()),
        out_specs=(
            P("space", None, None),
            P("embryo", "space", None, None),
            P("embryo", "space", None, None),
        ),
        check_vma=False,
    )
```

```python
import jax
import jax.numpy as jnp
import numpy as np
from jax import lax
from jax.experimental import pallas as pl
from jax.experimental.pallas import tpu as pltpu
from jax.sharding import PartitionSpec as P


ITERS = 3
RELAX = 0.8
REACH = 6
BF16 = jnp.bfloat16
F32 = jnp.float32


def tap_values():
    raw = np.exp(-np.arange(-REACH, REACH + 1, dtype=np.float64) ** 2 / 18.0)
    return raw / raw.sum()


TAPS = [float(v) for v in tap_values()[REACH:]]


def band(count):
    away = np.abs(np.arange(count)[:, None] - np.arange(count)[None, :])
    full = np.zeros((count, count))
    taps = tap_values()
    for shift in range(REACH + 1):
        full[away == shift] = taps[REACH + shift]
    return full.astype(np.float32)


def two_terms(matrix):
    high = jnp.asarray(matrix).astype(BF16)
    low = (jnp.asarray(matrix) - high.astype(F32)).astype(BF16)
    return high, low


def y_operand(count):
    high, low = two_terms(band(count))
    return jnp.concatenate([high, high, low], axis=1)


def z_operand(count):
    high, low = two_terms(band(count))
    row = jnp.concatenate([high, low], axis=1)
    return jnp.concatenate([row, row], axis=0)


def split(value):
    high = value.astype(BF16)
    return high, (value - high.astype(F32)).astype(BF16)


def x_pass(sources, stacked, rows, lanes):
    planes = len(sources) - 2 * REACH

    def step(tile, carry):
        at = pl.ds(pl.multiple_of(tile * 16, 16), 16)
        at_low = pl.ds(pl.multiple_of(tile * 16 + rows, 16), 16)
        load = lambda i: sources[i][0][sources[i][1], at, :]
        window = [load(i) for i in range(2 * REACH)]
        for p in range(planes):
            window.append(load(p + 2 * REACH))
            total = TAPS[0] * window[REACH]
            for shift in range(1, REACH + 1):
                total = total + TAPS[shift] * (window[REACH - shift] + window[REACH + shift])
            window.pop(0)
            high, low = split(total)
            stacked[at, p * lanes : (p + 1) * lanes] = high
            stacked[at_low, p * lanes : (p + 1) * lanes] = low
        return carry

    lax.fori_loop(0, rows // 16, step, 0)


def yz_plane_pair(stacked, by, bz, pair, lanes):
    rows = stacked.shape[0] // 2
    both = stacked[:, pair * 2 * lanes : (pair + 1) * 2 * lanes]
    rhs = jnp.concatenate([both, both[:rows]], axis=0)
    mid = jnp.dot(by[...], rhs, preferred_element_type=F32)
    out = []
    for half in range(2):
        high, low = split(mid[:, half * lanes : (half + 1) * lanes])
        wide = jnp.dot(jnp.concatenate([high, low], axis=1), bz[...], preferred_element_type=F32)
        out.append(wide[:, :lanes] + wide[:, lanes:])
    return out


ANY = pl.BlockSpec(memory_space=pl.ANY)
SMEM = pl.BlockSpec(memory_space=pltpu.SMEM)
VMEM = pl.BlockSpec(memory_space=pltpu.VMEM)
DMA = pltpu.SemaphoreType.DMA
GRANT = 12 << 20


def around(center, other, halo):
    mirrored = [(halo, REACH - 1 - i) for i in range(REACH)]
    own = [(center, i) for i in range(center.shape[0])]
    inner = [(other, i) for i in range(REACH)]
    if center.shape[0] == REACH:
        return mirrored + own + inner
    return inner + own + mirrored


def first_kernel(center, other, halo, log_density, by, bz, first, *rest):
    edge, stacked = rest[:-1], rest[-1]
    count, rows, lanes = center.shape
    x_pass(around(center, other, halo), stacked, rows, lanes)
    for pair in range(count // 2):
        for half, marginal in enumerate(yz_plane_pair(stacked, by, bz, pair, lanes)):
            p = pair * 2 + half
            value = jnp.exp(RELAX * (log_density[p] - jnp.log(marginal)))
            first[p] = value
            if edge and p >= count - REACH:
                edge[0][p - count + REACH] = value


def turns(spot):
    x = spot[0] & 3
    mix, top = (x & 1) ^ (x >> 1), x >> 1
    return mix * 2 + top, top * 2 + mix


def image_kernel(spot, weights, center, other, halo, second, by, bz, *refs):
    pieces, log_image, stacked = refs[:4], refs[4], refs[5]
    count, rows, lanes = center.shape
    places = turns(spot)
    total = weights[0]
    for k in range(1, weights.shape[0]):
        total = total + weights[k]
    weight = jnp.full((1, lanes), weights[spot[0]], F32) / jnp.full((1, lanes), total, F32)
    x_pass(around(center, other, halo), stacked, rows, lanes)
    side_count, quarter = count // 2, rows // 4
    for pair in range(count // 2):
        for half, image in enumerate(yz_plane_pair(stacked, by, bz, pair, lanes)):
            log_image[pair * 2 + half] = jnp.log(image)
        for half in range(2):
            p = pair * 2 + half
            side = p // side_count
            for slot in range(4):
                at = pl.ds(pl.multiple_of((slot ^ places[side]) * quarter, quarter), quarter)
                out = slice((slot % 2) * quarter, (slot % 2 + 1) * quarter)
                value = weight * (jnp.log(second[p, at, :]) + log_image[p, at, :])
                pieces[side * 2 + slot // 2][p - side * side_count, out, :] = value


def second_kernel(last, spot, *refs):
    places = turns(spot)
    pieces, log_image, second, extra = refs[:4], refs[4], refs[5], refs[6:]
    count, rows, _ = second.shape
    side_count, quarter = count // 2, rows // 4
    for k, piece in enumerate(pieces):
        side, which = k // 2, k % 2
        for i in range(side_count):
            p = side * side_count + i
            for b in range(2):
                at = pl.ds(pl.multiple_of(((which * 2 + b) ^ places[side]) * quarter, quarter), quarter)
                logmean = piece[i, b * quarter : (b + 1) * quarter, :]
                value = jnp.exp(RELAX * (logmean - log_image[p, at, :]))
                second[p, at, :] = value
                if last:
                    extra[0][p, at, :] = jnp.exp(logmean)
                elif extra and p >= count - REACH:
                    extra[0][p - count + REACH, at, :] = value


def placed(core, d, planes):
    return core[0] * (planes - 1 - d) + (1 - core[0]) * d


def split_kernel(logs, core, whole, *outs):
    planes = whole.shape[0]
    for out, low in zip(outs, (REACH, 0, planes - REACH)):

        def step(i, carry):
            cells = whole[placed(core, low + i, planes)]
            out[i] = jnp.log(cells) if logs else cells
            return carry

        lax.fori_loop(0, out.shape[0], step, 0)


def join_kernel(core, *refs):
    sems = refs[-1]
    n = (len(refs) - 1) // 3
    parts, wholes = refs[: 2 * n], refs[2 * n : 3 * n]
    planes = wholes[0].shape[0]
    copies = []
    for k, whole in enumerate(wholes):
        for part, low in zip(parts[2 * k : 2 * k + 2], (REACH, 0)):
            for i in range(part.shape[0]):
                target = whole.at[placed(core, low + i, planes)]
                copies.append(pltpu.make_async_copy(part.at[i], target, sems.at[k, low + i]))
                copies[-1].start()
    for copy in copies:
        copy.wait()


def body(density, scaling, weights):
    density, scaling = density[0], scaling[0]
    planes, rows, lanes = density.shape
    shape = lambda p, r=rows: jax.ShapeDtypeStruct((p, r, lanes), F32)
    main_count = planes - REACH
    by, bz = y_operand(rows), z_operand(lanes)
    count = lax.axis_size("space")
    core = (lax.axis_index("space") % 2).astype(jnp.int32)[None]
    spot = lax.axis_index("embryo").astype(jnp.int32)[None]
    params = pltpu.CompilerParams(vmem_limit_bytes=GRANT)

    def cost(p, flops, passes, exps):
        cells = p * rows * lanes
        return pl.CostEstimate(flops=cells * flops, bytes_accessed=cells * 4 * passes, transcendentals=cells * exps)

    def stacked(p):
        return [pltpu.VMEM((2 * rows, p * lanes), BF16)]

    def first_call(center, other, halo, log_density):
        p = center.shape[0]
        edge = (shape(REACH),) if p != REACH else ()
        return pl.pallas_call(
            first_kernel,
            out_shape=(shape(p),) + edge,
            in_specs=[VMEM] * 6,
            out_specs=(VMEM,) * (1 + len(edge)),
            scratch_shapes=stacked(p),
            compiler_params=params,
            cost_estimate=cost(p, 3000, 4, 3),
            name="first",
        )(center, other, halo, log_density, by, bz)

    def image_call(center, other, halo, second):
        p = center.shape[0]
        *pieces, log_image = pl.pallas_call(
            image_kernel,
            out_shape=(shape(p // 2, rows // 2),) * 4 + (shape(p),),
            in_specs=[SMEM] * 2 + [VMEM] * 6,
            out_specs=(VMEM,) * 5,
            scratch_shapes=stacked(p),
            compiler_params=params,
            cost_estimate=cost(p, 3000, 4, 3),
            name="image",
        )(spot, weights, center, other, halo, second, by, bz)
        return pieces, log_image

    def second_call(last, held, more, log_image):
        p = log_image.shape[0]
        extra = (shape(p),) if last else (shape(REACH),) if p != REACH else ()
        return pl.pallas_call(
            lambda *refs: second_kernel(last, *refs),
            out_shape=(shape(p),) + extra,
            in_specs=[SMEM] + [VMEM] * 5,
            out_specs=(VMEM,) * (1 + len(extra)),
            compiler_params=params,
            cost_estimate=cost(p, 4, 3, 1),
            name="last" if last else "second",
        )(spot, held[0], more[0], held[1], more[1], log_image)

    def split_call(logs, whole):
        outs = (shape(main_count), shape(REACH)) + (() if logs else (shape(REACH),))
        return pl.pallas_call(
            lambda *refs: split_kernel(logs, *refs),
            out_shape=outs,
            in_specs=[SMEM, VMEM],
            out_specs=(VMEM,) * len(outs),
            compiler_params=params,
            cost_estimate=cost(planes, 1, 2, 1),
            name="split",
        )(core, whole)

    def join_call(*parts):
        n = len(parts) // 2
        return pl.pallas_call(
            join_kernel,
            out_shape=(shape(planes),) * n,
            in_specs=[SMEM] + [VMEM] * len(parts),
            out_specs=(ANY,) * n,
            scratch_shapes=[DMA((n, planes))],
            compiler_params=params,
            cost_estimate=cost(planes, 1, 2 * n, 0),
            name="join",
        )(core, *parts)

    far_pairs = [(i, i + 1) for i in range(1, count - 1, 2)]
    near_pairs = [(i, i + 1) for i in range(0, count, 2)]

    def trade(value, pairs):
        return lax.ppermute(value, "space", pairs + [(b, a) for a, b in pairs])

    def partner_x(mask):
        return [(z * 4 + i, z * 4 + (i ^ mask)) for z in range(4) for i in range(4)]

    def partner_z(mask):
        return [(z * 4 + i, (z ^ mask) * 4 + i) for z in range(4) for i in range(4)]

    near_x, wrap_x = (partner_x(1), partner_x(3)), (partner_x(3), partner_x(1))
    near_z, wrap_z = (partner_z(1), partner_z(3)), (partner_z(3), partner_z(1))

    def swap(values, perms):
        values = lax.optimization_barrier(values)
        return lax.optimization_barrier([lax.ppermute(v, "embryo", p) for v, p in zip(values, perms)])

    def rest_of_sum(pieces, got):
        held = [k + g for k, g in zip(pieces[0::2], got)]
        mid = held[0].shape[1] // 2
        got = swap([v[:, mid:] for v in held], wrap_x)
        held = [v[:, :mid] + g for v, g in zip(held, got)]
        held = [v + g for v, g in zip(held, swap(held, near_z))]
        held = [v + g for v, g in zip(held, swap(held, wrap_z))]
        got = swap(held, wrap_x)
        held = [jnp.concatenate([v, g], axis=1) for v, g in zip(held, got)]
        return held, swap(held, near_x)

    def sweep(state, split_density, last):
        second_main, second_far, edge, density_parts = state
        far = trade(second_far, far_pairs)
        near = trade(edge, near_pairs)
        if split_density:
            density_parts = split_call(True, density)
        density_main, density_far = density_parts
        first_main, edge = first_call(second_main, second_far, near, density_main)
        near = trade(edge, near_pairs)
        (first_far,) = first_call(second_far, second_main, far, density_far)
        far = trade(first_far, far_pairs)
        pieces_main, log_main = image_call(first_main, first_far, near, second_main)
        got_main = swap(pieces_main[1::2], near_x)
        pieces_far, log_far = image_call(first_far, first_main, far, second_far)
        got_main, pieces_far = lax.optimization_barrier((got_main, pieces_far))
        got_far = swap(pieces_far[1::2], near_x)
        held_main, more_main = rest_of_sum(pieces_main, got_main)
        held_far, more_far = rest_of_sum(pieces_far, got_far)
        more_main, more_far = lax.optimization_barrier((more_main, more_far))
        second_far, *extra_far = second_call(last, held_far, more_far, log_far)
        second_main, *extra = second_call(last, held_main, more_main, log_main)
        return (second_main, second_far, extra[0], density_parts), extra_far, (first_main, first_far)

    state = (*split_call(False, scaling), None)
    for index in range(ITERS):
        state, extra_far, first_parts = sweep(state, index == 0, index == ITERS - 1)
    second_main, second_far, mean_main, _ = state
    (first,) = join_call(*first_parts)
    second, mean = join_call(second_main, second_far, mean_main, *extra_far)
    return mean, first[None], second[None]


def solution(mesh):
    return jax.shard_map(
        body,
        mesh=mesh,
        in_specs=(P("embryo", "space", None, None), P("embryo", "space", None, None), P()),
        out_specs=(
            P("space", None, None),
            P("embryo", "space", None, None),
            P("embryo", "space", None, None),
        ),
        check_vma=False,
    )
```
